32 devices in a mesh: grp: 2 (over y), img: 4 (over z), gz: 4 (over x, core).
Axes of the slice: x: 2, y: 2, z: 4, core: 2. Of those that a mesh axis runs over, the one named last changes fastest.
Arguments:
- ordering_variable: bfloat16 [16, 16, 64, 256], P(('grp', 'img'), 'gz'), parts along dimension 0, may hold values from 0 to 1
- lattice_shift_field: bfloat16 [3, 16, 16, 64, 256], P(None, ('grp', 'img'), 'gz'), parts along dimension 1, may hold values from -3 to 3
- eigenstrain_mismatch: float32 [2], P('grp'), parts along dimension 0, may hold values from 0.3 to 1
- thermal_state_kelvin: float32 [2], P('grp'), parts along dimension 0, may hold values from 1100 to 1300
Outputs:
- string: bfloat16 [16, 16, 64, 256], P(('grp', 'img'), 'gz'), parts along dimension 0
- moved: bfloat16 [3, 16, 16, 64, 256], P(None, ('grp', 'img'), 'gz'), parts along dimension 1
The draws below stay inside these ranges and needn't reach their ends.
There are 2 independent parts, one for each index of `grp`. The reference program is written for one: setup_inputs(seed, part) draws one part's arguments, and reference() takes and returns one part's arrays. A program takes and returns all parts, laid end to end along the dimension named above; each array names one. Nothing has to cross between parts.
All inputs are finite; a program needn't handle non-finite values.
Results may differ from the reference program's by a relative error of at most 0.0046.
Values may be sent and summed in bfloat16 or wider, within the bound.
A program may use at most 64 MiB of HBM per device.

```python
import math
import jax
import jax.numpy as jnp
from jax import lax

NX = 64
NY = 256
IMAGES = 8
NZ = 16


def draw_ordering_variable(key, part):
    folded_key = jax.random.fold_in(key, 17)
    step_key, first_key, second_random_key, jitter_key = jax.random.split(folded_key, 4)
    steps_log = jax.random.uniform(step_key, (IMAGES - 1,), jnp.float32, math.log(0.2), math.log(5.0))
    increments = jnp.exp(steps_log)
    progress = jnp.concatenate([jnp.zeros((1,), jnp.float32), jnp.cumsum(increments)]) / jnp.sum(increments)
    height = jnp.arange(NZ, dtype=jnp.float32) / max(NZ - 1, 1)
    first_field = jax.random.uniform(first_key, (NZ, NX, NY), jnp.float32)
    second_field = jax.random.uniform(second_random_key, (NZ, NX, NY), jnp.float32)
    profile = 0.35 + 0.65 * height
    weight_first = progress[:, None, None, None]
    blended = weight_first * first_field[None] + (1.0 - weight_first) * second_field[None]
    jitter_field = jax.random.uniform(jitter_key, (IMAGES, NZ, NX, NY), jnp.float32, -0.02, 0.02)
    return jnp.clip(profile[None, :, None, None] * blended + jitter_field, 0.0, 1.0).astype(jnp.bfloat16)


def block_scale(rng, shape, pieces, least, top_value):
    def one(axis_at, parts):
        steps = jax.random.uniform(jax.random.fold_in(jax.random.fold_in(rng, 6), axis_at), (parts,), jnp.float32, least / len(pieces), top_value / len(pieces))
        return jnp.repeat(jnp.exp(steps), shape[axis_at] // parts).reshape((-1,) + (1,) * (len(shape) - axis_at - 1))

    gain = one(*pieces[0])
    for cut in pieces[1:]:
        gain = gain * one(*cut)
    return gain


def scatter_about(rng, extent, scale, most, cuts=(), held_as=jnp.bfloat16):
    result = scale * jax.random.normal(rng, extent, jnp.float32)
    if cuts:
        result = result * block_scale(rng, extent, cuts, -0.22, 0.18)
    return jnp.clip(result, -most, most).astype(held_as)


def setup_inputs(seed: int = 0, part: int = 0) -> dict:
    key_list = jax.random.split(jax.random.key(seed), 5)
    own_keys = jax.random.split(jax.random.fold_in(key_list[4], part), 5)
    return {
        "ordering_variable": draw_ordering_variable(jax.random.fold_in(jax.random.fold_in(key_list[4], part), 71), part),
        "lattice_shift_field": scatter_about(own_keys[1], (3, IMAGES, NZ, NX, NY), 0.5, 3.0, ((1, 4), (2, 4))),
        "eigenstrain_mismatch": jnp.clip(jnp.exp(jax.random.uniform(own_keys[2], (1,), jnp.float32, math.log(0.3), math.log(1.0))), 0.3, 1.0),
        "thermal_state_kelvin": jnp.clip(jax.random.uniform(own_keys[3], (1,), jnp.float32, 1100.0, 1300.0), 1100.0, 1300.0),
    }


stiff_eleven = 2.5
stiff_twelve = 1.5
stiff_shear = 1.2
barrier = 1.0
latent_enthalpy = 8.0
dissolution_limit_kelvin = 1250.0
gradient_coef = 1.0
mobility = 0.1
elastic_step = 0.03
epsilon = 1e-06

def switching(value):
    return value * value * (3.0 - 2.0 * value)

def switching_slope(value):
    return 6.0 * value * (1.0 - value)

def well_slope(value):
    return 2.0 * value * (1.0 - value) * (1.0 - 2.0 * value)

def cubic_stress(slopes, eigen):
    strain_xx = slopes[0] + eigen
    strain_yy = slopes[1] + eigen
    strain_zz = slopes[2] + eigen
    return (stiff_eleven * strain_xx + stiff_twelve * (strain_yy + strain_zz), stiff_eleven * strain_yy + stiff_twelve * (strain_xx + strain_zz), stiff_eleven * strain_zz + stiff_twelve * (strain_xx + strain_yy), stiff_shear * (slopes[3] + slopes[4]), stiff_shear * (slopes[5] + slopes[6]), stiff_shear * (slopes[7] + slopes[8]))

def forward_step(field, axis):
    return jnp.roll(field, -1, axis) - field

def backward_step(field, axis):
    return field - jnp.roll(field, 1, axis)

def relax_image(order_half, shift_half, misfit_value, chemical_free_energy_gain):
    order = order_half.astype(jnp.float32)
    shifts = shift_half.astype(jnp.float32)
    homogeneous = misfit_value * jnp.mean(switching(order))
    eigen = homogeneous - misfit_value * switching(order)
    along_x = shifts[0]
    along_y = shifts[1]
    along_z = shifts[2]
    slopes = (forward_step(along_x, 1), forward_step(along_y, 2), forward_step(along_z, 0), forward_step(along_y, 1), forward_step(along_x, 2), forward_step(along_z, 1), forward_step(along_x, 0), forward_step(along_z, 2), forward_step(along_y, 0))
    stress = cubic_stress(slopes, eigen)
    force = jnp.stack([backward_step(stress[0], 1) + backward_step(stress[3], 2) + backward_step(stress[4], 0), backward_step(stress[3], 1) + backward_step(stress[1], 2) + backward_step(stress[5], 0), backward_step(stress[4], 1) + backward_step(stress[5], 2) + backward_step(stress[2], 0)])
    moved = (shifts + elastic_step * force).astype(jnp.bfloat16)
    laplace = jnp.roll(order, 1, 0) + jnp.roll(order, -1, 0) + (jnp.roll(order, 1, 1) + jnp.roll(order, -1, 1)) + (jnp.roll(order, 1, 2) + jnp.roll(order, -1, 2)) - 6.0 * order
    potential = barrier * well_slope(order) + chemical_free_energy_gain * switching_slope(order) - gradient_coef * laplace - misfit_value * switching_slope(order) * (stress[0] + stress[1] + stress[2])
    relaxed = (order - mobility * potential).astype(jnp.bfloat16)
    return (relaxed, moved)

def reference(ordering_variable, lattice_shift_field, eigenstrain_mismatch, thermal_state_kelvin):
    misfit_value = eigenstrain_mismatch[0]
    chemical_free_energy_gain = latent_enthalpy * (thermal_state_kelvin[0] - dissolution_limit_kelvin) / dissolution_limit_kelvin

    def one_image(pair):
        return relax_image(pair[0], pair[1], misfit_value, chemical_free_energy_gain)
    relaxed, moved = lax.map(one_image, (ordering_variable, jnp.moveaxis(lattice_shift_field, 1, 0)))
    moved = jnp.moveaxis(moved, 0, 1)
    images = relaxed.shape[0]
    current = relaxed.astype(jnp.float32)

    def one_gap(pair):
        return jnp.sqrt(jnp.mean((pair[1] - pair[0]) ** 2) + epsilon)
    gaps = lax.map(one_gap, (current[:-1], current[1:]))
    single = jnp.ones((1,), jnp.float32)
    arc = jnp.concatenate([jnp.zeros((1,), jnp.float32), jnp.cumsum(gaps)])
    target = arc[-1] * (jnp.arange(images, dtype=jnp.float32) / (images - 1))
    below_gap = jnp.concatenate([single, gaps])
    above_gap = jnp.concatenate([gaps, single])
    back = jnp.clip((arc - target) / below_gap, 0.0, 1.0)
    ahead = jnp.clip((target - arc) / above_gap, 0.0, 1.0)
    blank = jnp.zeros_like(current[:1])
    previous = jnp.concatenate([blank, current[:-1]])
    following = jnp.concatenate([current[1:], blank])
    string = (current + ahead[:, None, None, None] * (following - current) + back[:, None, None, None] * (previous - current)).astype(jnp.bfloat16)
    return (string, moved)
```

```python
import functools

import jax
import jax.numpy as jnp
from jax import lax
from jax.experimental import pallas as pl
from jax.experimental.pallas import tpu as pltpu
from jax.sharding import PartitionSpec as P

stiff_eleven = 2.5
stiff_twelve = 1.5
stiff_shear = 1.2
barrier_height = 1.0
latent_enthalpy = 8.0
dissolution_limit_kelvin = 1250.0
gradient_coef = 1.0
mobility = 0.1
elastic_step = 0.03
epsilon = 1e-06
LANES = 128
MESH = pl.DeviceIdType.MESH


def switching(value):
    return value * value * (3.0 - 2.0 * value)


def roll(field, shift, axis):
    return pltpu.roll(field, shift % field.shape[axis], axis)


def ahead_of(field, axis):
    return roll(field, -1, axis) - field


def behind_of(field, axis):
    return field - roll(field, 1, axis)


def lane_row(field):
    row = jnp.sum(field, axis=0, keepdims=True)
    out = row[:, :LANES]
    for start in range(LANES, row.shape[1], LANES):
        out = out + row[:, start : start + LANES]
    return out


def kernel(
    n_img,
    n_gz,
    misfit_ref,
    kelvin_ref,
    order_in,
    shift_in,
    string_ref,
    moved_ref,
    obuf,
    sbuf,
    rbuf,
    hbuf,
    gbuf,
    load_sem,
    halo_send,
    halo_recv,
    image_send,
    image_recv,
    h_send,
    h_recv,
    g_send,
    g_recv,
):
    images, planes, nx, ny = order_in.shape
    cells = float(planes * n_gz * nx * ny)
    img = lax.axis_index("img")
    gz = lax.axis_index("gz")
    n_all = n_img * n_gz
    me = img * n_gz + gz
    above, below = lax.rem(gz + 1, n_gz), lax.rem(gz + n_gz - 1, n_gz)

    loads = [
        pltpu.make_async_copy(order_in, obuf.at[:, 1 : planes + 1], load_sem.at[0]),
        pltpu.make_async_copy(shift_in, sbuf.at[:, :, 1 : planes + 1], load_sem.at[1]),
    ]
    for load in loads:
        load.start()

    barrier = pltpu.get_barrier_semaphore()

    def greet(step, carry):
        other = lax.rem(me + step, n_all)
        pl.semaphore_signal(
            barrier,
            inc=1,
            device_id={"img": other // n_gz, "gz": lax.rem(other, n_gz)},
            device_id_type=MESH,
        )
        return carry

    lax.fori_loop(1, n_all, greet, 0)
    pl.semaphore_wait(barrier, n_all - 1)

    def halo(slot, source, target, neighbour):
        return pltpu.make_async_remote_copy(
            src_ref=source,
            dst_ref=target,
            send_sem=halo_send.at[slot],
            recv_sem=halo_recv.at[slot],
            device_id={"gz": neighbour},
            device_id_type=MESH,
        )

    last, top = planes - 1, planes + 1
    order_down = halo(0, order_in.at[:, 0], obuf.at[:, top], below)
    order_up = halo(1, order_in.at[:, last], obuf.at[:, 0], above)
    lift_down = halo(2, shift_in.at[2, :, 0], sbuf.at[2, :, top], below)
    shift_up = halo(3, shift_in.at[:, :, last], sbuf.at[:, :, 0], above)
    flat_down = halo(4, shift_in.at[0:2, :, 0], sbuf.at[0:2, :, top], below)
    first_halos = (order_down, order_up, lift_down)
    later_halos = (shift_up, flat_down)
    for copy in first_halos + later_halos:
        copy.start()

    misfit = misfit_ref[0]
    drive = latent_enthalpy * (kelvin_ref[0] - dissolution_limit_kelvin) / dissolution_limit_kelvin

    def order_at(l, z):
        return obuf[l, z].astype(jnp.float32)

    def shift_at(c, l, z):
        return sbuf[c, l, z].astype(jnp.float32)

    loads[0].wait()
    for l in range(images):

        def add_h(z, total, l=l):
            return total + lane_row(switching(order_at(l, z + 1)))

        hbuf[gz, l : l + 1] = lax.fori_loop(0, planes, add_h, jnp.zeros((1, LANES), jnp.float32))

    def h_copy(step):
        return pltpu.make_async_remote_copy(
            src_ref=hbuf.at[gz],
            dst_ref=hbuf.at[gz],
            send_sem=h_send.at[step],
            recv_sem=h_recv.at[step],
            device_id={"gz": lax.rem(gz + step, n_gz)},
            device_id_type=MESH,
        )

    def h_arrival(step):
        origin = lax.rem(gz + n_gz - step, n_gz)
        return pltpu.make_async_remote_copy(
            src_ref=hbuf.at[origin],
            dst_ref=hbuf.at[origin],
            send_sem=h_send.at[step],
            recv_sem=h_recv.at[step],
            device_id={"gz": origin},
            device_id_type=MESH,
        )

    for step in range(1, n_gz):
        h_copy(step).start()

    def move_plane(l, z):
        ux, uy, uz = shift_at(0, l, z + 1), shift_at(1, l, z + 1), shift_at(2, l, z + 1)
        vx, vy, vz = shift_at(0, l, z), shift_at(1, l, z), shift_at(2, l, z)
        zx = shift_at(0, l, z + 2) - ux
        zy = shift_at(1, l, z + 2) - uy
        zz = shift_at(2, l, z + 2) - uz
        dx, dy, dz = ux - vx, uy - vy, uz - vz
        total = stiff_eleven + 2.0 * stiff_twelve
        swell = (-total * misfit) * switching(order_at(l, z + 1))
        swell_under = (-total * misfit) * switching(order_at(l, z))
        xx, yy = ahead_of(ux, 0), ahead_of(uy, 1)
        s_xx = stiff_eleven * xx + stiff_twelve * (yy + zz) + swell
        s_yy = stiff_eleven * yy + stiff_twelve * (xx + zz) + swell
        s_xy = stiff_shear * (ahead_of(uy, 0) + ahead_of(ux, 1))
        s_xz = stiff_shear * (ahead_of(uz, 0) + zx)
        s_yz = stiff_shear * (ahead_of(uz, 1) + zy)
        f_x = behind_of(s_xx, 0) + behind_of(s_xy, 1)
        f_x = f_x + stiff_shear * (ahead_of(dz, 0) + (zx - dx))
        moved_ref[0, l, z] = (ux + elastic_step * f_x).astype(jnp.bfloat16)
        f_y = behind_of(s_xy, 0) + behind_of(s_yy, 1)
        f_y = f_y + stiff_shear * (ahead_of(dz, 1) + (zy - dy))
        moved_ref[1, l, z] = (uy + elastic_step * f_y).astype(jnp.bfloat16)
        f_z = behind_of(s_xz, 0) + behind_of(s_yz, 1)
        f_z = f_z + stiff_eleven * (zz - dz)
        f_z = f_z + stiff_twelve * (ahead_of(dx, 0) + ahead_of(dy, 1)) + (swell - swell_under)
        moved_ref[2, l, z] = (uz + elastic_step * f_z).astype(jnp.bfloat16)

    def relax_plane(l, z, homogeneous):
        order = order_at(l, z + 1)
        uz = shift_at(2, l, z + 1)
        divergence = ahead_of(shift_at(0, l, z + 1), 0) + ahead_of(shift_at(1, l, z + 1), 1)
        divergence = divergence + (shift_at(2, l, z + 2) - uz)
        eigen = homogeneous - misfit * switching(order)
        trace = (stiff_eleven + 2.0 * stiff_twelve) * (divergence + 3.0 * eigen)
        laplace = order_at(l, z) + order_at(l, z + 2)
        laplace = laplace + (roll(order, 1, 0) + roll(order, -1, 0))
        laplace = laplace + (roll(order, 1, 1) + roll(order, -1, 1)) - 6.0 * order
        bend = order * (1.0 - order)
        potential = (
            bend * (barrier_height * 2.0 * (1.0 - 2.0 * order) + 6.0 * (drive - misfit * trace))
            - gradient_coef * laplace
        )
        rbuf[l + 1, z] = (order - mobility * potential).astype(jnp.bfloat16)

    inner = planes - 2

    def inner_planes(work):
        def one(step, carry):
            work(step // inner, lax.rem(step, inner) + 1)
            return carry

        lax.fori_loop(0, images * inner, one, 0)

    def outer_planes(work):
        def one(step, carry):
            work(step // 2, lax.rem(step, 2) * last)
            return carry

        lax.fori_loop(0, images * 2, one, 0)

    loads[1].wait()
    inner_planes(move_plane)

    for step in range(1, n_gz):
        h_arrival(step).wait_recv()
    h_sum = jnp.sum(jnp.sum(hbuf[...], axis=0), axis=-1, keepdims=True)
    h_mean = misfit * (h_sum / cells)

    def relax(l, z):
        picked = jnp.where(lax.broadcasted_iota(jnp.int32, (images, 1), 0) == l, h_mean, 0.0)
        relax_plane(l, z, jnp.sum(picked, axis=0, keepdims=True))

    inner_planes(relax)

    has_next = img < n_img - 1
    has_previous = img > 0

    def image_copy(slot, span, forward):
        return pltpu.make_async_remote_copy(
            src_ref=rbuf.at[images if forward else 1, span],
            dst_ref=rbuf.at[0 if forward else images + 1, span],
            send_sem=image_send.at[slot],
            recv_sem=image_recv.at[slot],
            device_id={"img": img + 1 if forward else img - 1},
            device_id_type=MESH,
        )

    spans = (slice(1, last), slice(0, 1), slice(last, planes))
    forward_copies = [image_copy(i, span, True) for i, span in enumerate(spans)]
    backward_copies = [image_copy(3 + i, span, False) for i, span in enumerate(spans)]

    def send_images(picks):
        @pl.when(has_previous)
        def _():
            for i in picks:
                backward_copies[i].start()

        @pl.when(has_next)
        def _():
            for i in picks:
                forward_copies[i].start()

    send_images((0,))

    @pl.when(jnp.logical_not(has_previous))
    def _():
        rbuf[0] = jnp.zeros_like(rbuf[0])

    @pl.when(jnp.logical_not(has_next))
    def _():
        rbuf[images + 1] = jnp.zeros_like(rbuf[images + 1])

    for copy in first_halos:
        copy.wait_recv()
    outer_planes(relax)
    send_images((1, 2))

    def squares(l):
        def add(z, total):
            step = rbuf[l + 2, z].astype(jnp.float32) - rbuf[l + 1, z].astype(jnp.float32)
            return total + lane_row(step * step)

        gbuf[me, l : l + 1] = lax.fori_loop(0, planes, add, jnp.zeros((1, LANES), jnp.float32))

    for l in range(images - 1):
        squares(l)

    @pl.when(has_next)
    def _():
        for copy in backward_copies:
            copy.wait_recv()

    squares(images - 1)

    def place(index):
        return {"img": index // n_gz, "gz": lax.rem(index, n_gz)}

    def g_copy(step):
        return pltpu.make_async_remote_copy(
            src_ref=gbuf.at[me],
            dst_ref=gbuf.at[me],
            send_sem=g_send.at[step],
            recv_sem=g_recv.at[step],
            device_id=place(lax.rem(me + step, n_all)),
            device_id_type=MESH,
        )

    def g_arrival(step):
        origin = lax.rem(me + n_all - step, n_all)
        return pltpu.make_async_remote_copy(
            src_ref=gbuf.at[origin],
            dst_ref=gbuf.at[origin],
            send_sem=g_send.at[step],
            recv_sem=g_recv.at[step],
            device_id=place(origin),
            device_id_type=MESH,
        )

    def g_start(step, carry):
        g_copy(step).start()
        return carry

    lax.fori_loop(1, n_all, g_start, 0)

    for copy in later_halos:
        copy.wait_recv()
    outer_planes(move_plane)

    @pl.when(has_previous)
    def _():
        for copy in forward_copies:
            copy.wait_recv()

    def g_wait(step, carry):
        g_arrival(step).wait_recv()
        return carry

    lax.fori_loop(1, n_all, g_wait, 0)

    total_images = images * n_img
    gaps = []
    for i in range(n_img):
        part = jnp.sum(gbuf[i * n_gz : (i + 1) * n_gz], axis=0)
        part = jnp.sum(part, axis=-1, keepdims=True)
        gaps.append(jnp.sqrt(part / cells + epsilon))

    def pick(low, high):
        out = jnp.zeros((1, 1), jnp.float32)
        for i in range(n_img):
            row = lax.broadcasted_iota(jnp.int32, (images, 1), 0) + i * images
            chosen = jnp.where((row >= low) & (row < high), gaps[i], 0.0)
            out = out + jnp.sum(chosen, axis=0, keepdims=True)
        return out

    length = pick(0, total_images - 1)
    for l in range(images):
        position = img * images + l
        arc = pick(0, position)
        target = length * (position.astype(jnp.float32) / (total_images - 1))
        gap_under = jnp.where(position == 0, 1.0, pick(position - 1, position))
        gap_over = jnp.where(position == total_images - 1, 1.0, pick(position, position + 1))
        back = jnp.clip((arc - target) / gap_under, 0.0, 1.0)
        ahead = jnp.clip((target - arc) / gap_over, 0.0, 1.0)

        def blend(z, carry, l=l, back=back, ahead=ahead):
            current = rbuf[l + 1, z].astype(jnp.float32)
            following = rbuf[l + 2, z].astype(jnp.float32)
            previous = rbuf[l, z].astype(jnp.float32)
            string_ref[l, z] = (
                current + ahead * (following - current) + back * (previous - current)
            ).astype(jnp.bfloat16)
            return carry

        lax.fori_loop(0, planes, blend, 0)

    for copy in first_halos + later_halos:
        copy.wait_send()
    for step in range(1, n_gz):
        h_copy(step).wait_send()

    @pl.when(has_previous)
    def _():
        for copy in backward_copies:
            copy.wait_send()

    @pl.when(has_next)
    def _():
        for copy in forward_copies:
            copy.wait_send()

    def g_done(step, carry):
        g_copy(step).wait_send()
        return carry

    lax.fori_loop(1, n_all, g_done, 0)


def shards(ordering_variable, lattice_shift_field, eigenstrain_mismatch, thermal_state_kelvin):
    n_img, n_gz = lax.axis_size("img"), lax.axis_size("gz")
    images, planes, nx, ny = ordering_variable.shape
    dma = pltpu.SemaphoreType.DMA
    return pl.pallas_call(
        functools.partial(kernel, n_img, n_gz),
        out_shape=(
            jax.ShapeDtypeStruct(ordering_variable.shape, jnp.bfloat16),
            jax.ShapeDtypeStruct(lattice_shift_field.shape, jnp.bfloat16),
        ),
        in_specs=[
            pl.BlockSpec(memory_space=pltpu.SMEM),
            pl.BlockSpec(memory_space=pltpu.SMEM),
            pl.BlockSpec(memory_space=pl.ANY),
            pl.BlockSpec(memory_space=pl.ANY),
        ],
        out_specs=(
            pl.BlockSpec(memory_space=pltpu.VMEM),
            pl.BlockSpec(memory_space=pltpu.VMEM),
        ),
        scratch_shapes=[
            pltpu.VMEM((images, planes + 2, nx, ny), jnp.bfloat16),
            pltpu.VMEM((3, images, planes + 2, nx, ny), jnp.bfloat16),
            pltpu.VMEM((images + 2, planes, nx, ny), jnp.bfloat16),
            pltpu.VMEM((n_gz, images, LANES), jnp.float32),
            pltpu.VMEM((n_img * n_gz, images, LANES), jnp.float32),
            dma((2,)),
            dma((5,)),
            dma((5,)),
            dma((6,)),
            dma((6,)),
            dma((n_gz,)),
            dma((n_gz,)),
            dma((n_img * n_gz,)),
            dma((n_img * n_gz,)),
        ],
        compiler_params=pltpu.CompilerParams(
            collective_id=0, has_side_effects=True, vmem_limit_bytes=24 * 1024 * 1024
        ),
    )(eigenstrain_mismatch, thermal_state_kelvin, ordering_variable, lattice_shift_field)


def solution(mesh):
    in_specs = (
        P(("grp", "img"), "gz", None, None),
        P(None, ("grp", "img"), "gz", None, None),
        P("grp"),
        P("grp"),
    )
    out_specs = (P(("grp", "img"), "gz", None, None), P(None, ("grp", "img"), "gz", None, None))
    return jax.shard_map(shards, mesh=mesh, in_specs=in_specs, out_specs=out_specs, check_vma=False)
```

```python
import functools

import jax
import jax.numpy as jnp
from jax import lax
from jax.experimental import pallas as pl
from jax.experimental.pallas import tpu as pltpu
from jax.sharding import PartitionSpec as P

stiff_eleven = 2.5
stiff_twelve = 1.5
stiff_shear = 1.2
barrier_height = 1.0
latent_enthalpy = 8.0
dissolution_limit_kelvin = 1250.0
gradient_coef = 1.0
mobility = 0.1
elastic_step = 0.03
epsilon = 1e-06
LANES = 128
MESH = pl.DeviceIdType.MESH


def switching(value):
    return value * value * (3.0 - 2.0 * value)


def roll(field, shift, axis):
    return pltpu.roll(field, shift % field.shape[axis], axis)


def ahead_of(field, axis):
    return roll(field, -1, axis) - field


def behind_of(field, axis):
    return field - roll(field, 1, axis)


def lane_row(field):
    row = jnp.sum(field, axis=0, keepdims=True)
    out = row[:, :LANES]
    for start in range(LANES, row.shape[1], LANES):
        out = out + row[:, start : start + LANES]
    return out


def kernel(
    n_img,
    n_gz,
    misfit_ref,
    kelvin_ref,
    order_in,
    shift_in,
    rbuf,
    moved_ref,
    weight_ref,
    obuf,
    sbuf,
    hbuf,
    gbuf,
    word_sem,
    load_sem,
    halo_send,
    halo_recv,
    image_send,
    image_recv,
    h_send,
    h_recv,
    g_send,
    g_recv,
):
    images, planes, nx, ny = order_in.shape
    cells = float(planes * n_gz * nx * ny)
    img = lax.axis_index("img")
    gz = lax.axis_index("gz")
    n_all = n_img * n_gz
    me = img * n_gz + gz
    above, below = lax.rem(gz + 1, n_gz), lax.rem(gz + n_gz - 1, n_gz)

    loads = [
        pltpu.make_async_copy(order_in, obuf.at[:, 1 : planes + 1], load_sem.at[0]),
        pltpu.make_async_copy(shift_in, sbuf.at[:, :, 1 : planes + 1], load_sem.at[1]),
    ]
    for load in loads:
        load.start()

    barrier = pltpu.get_barrier_semaphore()

    has_next = img < n_img - 1
    has_previous = img > 0
    n_near = has_next.astype(jnp.int32) + has_previous.astype(jnp.int32)

    def signal_near(sem):
        @pl.when(has_next)
        def _():
            pl.semaphore_signal(sem, inc=1, device_id={"img": img + 1}, device_id_type=MESH)

        @pl.when(has_previous)
        def _():
            pl.semaphore_signal(sem, inc=1, device_id={"img": img - 1}, device_id_type=MESH)

    for step in range(1, n_gz):
        pl.semaphore_signal(
            barrier,
            inc=1,
            device_id={"gz": lax.rem(gz + step, n_gz)},
            device_id_type=MESH,
        )
    signal_near(barrier)
    pl.semaphore_wait(barrier, n_gz - 1 + n_near)

    def spread(first, stop):
        for stage in range(first, stop):
            if stage > 0:
                pl.semaphore_wait(word_sem.at[stage - 1], n_near)
            if stage < n_img - 1:
                signal_near(word_sem.at[stage])

    def halo(slot, source, target, neighbour):
        return pltpu.make_async_remote_copy(
            src_ref=source,
            dst_ref=target,
            send_sem=halo_send.at[slot],
            recv_sem=halo_recv.at[slot],
            device_id={"gz": neighbour},
            device_id_type=MESH,
        )

    last, top = planes - 1, planes + 1
    order_down = halo(0, order_in.at[:, 0], obuf.at[:, top], below)
    order_up = halo(1, order_in.at[:, last], obuf.at[:, 0], above)
    lift_down = halo(2, shift_in.at[2, :, 0], sbuf.at[2, :, top], below)
    shift_up = halo(3, shift_in.at[:, :, last], sbuf.at[:, :, 0], above)
    flat_down = halo(4, shift_in.at[0:2, :, 0], sbuf.at[0:2, :, top], below)
    first_halos = (order_down, order_up, lift_down)
    later_halos = (shift_up, flat_down)
    for copy in first_halos:
        copy.start()
    spread(0, 1)

    misfit = misfit_ref[0]
    drive = latent_enthalpy * (kelvin_ref[0] - dissolution_limit_kelvin) / dissolution_limit_kelvin

    def order_at(l, z):
        return obuf[l, z].astype(jnp.float32)

    def shift_at(c, l, z):
        return sbuf[c, l, z].astype(jnp.float32)

    loads[0].wait()
    for l in range(images):

        def add_h(z, total, l=l):
            return total + lane_row(switching(order_at(l, z + 1)))

        hbuf[gz, l : l + 1] = lax.fori_loop(0, planes, add_h, jnp.zeros((1, LANES), jnp.float32))

    def h_copy(step):
        return pltpu.make_async_remote_copy(
            src_ref=hbuf.at[gz],
            dst_ref=hbuf.at[gz],
            send_sem=h_send.at[step],
            recv_sem=h_recv.at[step],
            device_id={"gz": lax.rem(gz + step, n_gz)},
            device_id_type=MESH,
        )

    def h_arrival(step):
        origin = lax.rem(gz + n_gz - step, n_gz)
        return pltpu.make_async_remote_copy(
            src_ref=hbuf.at[origin],
            dst_ref=hbuf.at[origin],
            send_sem=h_send.at[step],
            recv_sem=h_recv.at[step],
            device_id={"gz": origin},
            device_id_type=MESH,
        )

    for step in range(1, n_gz):
        h_copy(step).start()
    spread(1, 2)

    def move_plane(l, z):
        ux, uy, uz = shift_at(0, l, z + 1), shift_at(1, l, z + 1), shift_at(2, l, z + 1)
        vx, vy, vz = shift_at(0, l, z), shift_at(1, l, z), shift_at(2, l, z)
        zx = shift_at(0, l, z + 2) - ux
        zy = shift_at(1, l, z + 2) - uy
        zz = shift_at(2, l, z + 2) - uz
        dx, dy, dz = ux - vx, uy - vy, uz - vz
        total = stiff_eleven + 2.0 * stiff_twelve
        swell = (-total * misfit) * switching(order_at(l, z + 1))
        swell_under = (-total * misfit) * switching(order_at(l, z))
        xx, yy = ahead_of(ux, 0), ahead_of(uy, 1)
        s_xx = stiff_eleven * xx + stiff_twelve * (yy + zz) + swell
        s_yy = stiff_eleven * yy + stiff_twelve * (xx + zz) + swell
        s_xy = stiff_shear * (ahead_of(uy, 0) + ahead_of(ux, 1))
        s_xz = stiff_shear * (ahead_of(uz, 0) + zx)
        s_yz = stiff_shear * (ahead_of(uz, 1) + zy)
        f_x = behind_of(s_xx, 0) + behind_of(s_xy, 1)
        f_x = f_x + stiff_shear * (ahead_of(dz, 0) + (zx - dx))
        moved_ref[0, l, z] = (ux + elastic_step * f_x).astype(jnp.bfloat16)
        f_y = behind_of(s_xy, 0) + behind_of(s_yy, 1)
        f_y = f_y + stiff_shear * (ahead_of(dz, 1) + (zy - dy))
        moved_ref[1, l, z] = (uy + elastic_step * f_y).astype(jnp.bfloat16)
        f_z = behind_of(s_xz, 0) + behind_of(s_yz, 1)
        f_z = f_z + stiff_eleven * (zz - dz)
        f_z = f_z + stiff_twelve * (ahead_of(dx, 0) + ahead_of(dy, 1)) + (swell - swell_under)
        moved_ref[2, l, z] = (uz + elastic_step * f_z).astype(jnp.bfloat16)

    def relax_plane(l, z, homogeneous):
        order = order_at(l, z + 1)
        uz = shift_at(2, l, z + 1)
        divergence = ahead_of(shift_at(0, l, z + 1), 0) + ahead_of(shift_at(1, l, z + 1), 1)
        divergence = divergence + (shift_at(2, l, z + 2) - uz)
        eigen = homogeneous - misfit * switching(order)
        trace = (stiff_eleven + 2.0 * stiff_twelve) * (divergence + 3.0 * eigen)
        laplace = order_at(l, z) + order_at(l, z + 2)
        laplace = laplace + (roll(order, 1, 0) + roll(order, -1, 0))
        laplace = laplace + (roll(order, 1, 1) + roll(order, -1, 1)) - 6.0 * order
        bend = order * (1.0 - order)
        potential = (
            bend * (barrier_height * 2.0 * (1.0 - 2.0 * order) + 6.0 * (drive - misfit * trace))
            - gradient_coef * laplace
        )
        rbuf[l + 1, z] = (order - mobility * potential).astype(jnp.bfloat16)

    inner = planes - 2

    def inner_planes(work):
        def one(step, carry):
            work(step // inner, lax.rem(step, inner) + 1)
            return carry

        lax.fori_loop(0, images * inner, one, 0)

    def outer_planes(work):
        def one(step, carry):
            work(step // 2, lax.rem(step, 2) * last)
            return carry

        lax.fori_loop(0, images * 2, one, 0)

    loads[1].wait()
    spread(2, 3)

    for step in range(1, n_gz):
        h_arrival(step).wait_recv()
    h_sum = jnp.sum(jnp.sum(hbuf[...], axis=0), axis=-1, keepdims=True)
    h_mean = misfit * (h_sum / cells)

    def relax(l, z):
        relax_plane(l, z, h_mean[l : l + 1])

    for l in range(images):

        def relax_inner(z, carry, l=l):
            relax(l, z)
            return carry

        lax.fori_loop(1, last, relax_inner, 0)
    spread(3, n_img)

    def image_copy(slot, span, forward):
        return pltpu.make_async_remote_copy(
            src_ref=rbuf.at[images if forward else 1, span],
            dst_ref=rbuf.at[0 if forward else images + 1, span],
            send_sem=image_send.at[slot],
            recv_sem=image_recv.at[slot],
            device_id={"img": img + 1 if forward else img - 1},
            device_id_type=MESH,
        )

    spans = (slice(1, last), slice(0, 1), slice(last, planes))
    forward_copies = [image_copy(i, span, True) for i, span in enumerate(spans)]
    backward_copies = [image_copy(3 + i, span, False) for i, span in enumerate(spans)]

    def send_images(picks):
        @pl.when(has_previous)
        def _():
            for i in picks:
                backward_copies[i].start()

        @pl.when(has_next)
        def _():
            for i in picks:
                forward_copies[i].start()

    send_images((0,))

    @pl.when(jnp.logical_not(has_previous))
    def _():
        rbuf[0] = jnp.zeros_like(rbuf[0])

    @pl.when(jnp.logical_not(has_next))
    def _():
        rbuf[images + 1] = jnp.zeros_like(rbuf[images + 1])

    inner_planes(move_plane)

    order_up.wait_recv()
    for l in range(images):
        relax(l, 0)
    send_images((1,))
    order_down.wait_recv()
    lift_down.wait_recv()
    for copy in later_halos:
        copy.start()
    for l in range(images):
        relax(l, last)
    send_images((2,))

    def squares(l, first, stop, total):
        def add(z, total):
            step = rbuf[l + 2, z].astype(jnp.float32) - rbuf[l + 1, z].astype(jnp.float32)
            return total + lane_row(step * step)

        return lax.fori_loop(first, stop, add, total)

    nothing = jnp.zeros((1, LANES), jnp.float32)
    for l in range(images - 1):
        gbuf[me, l : l + 1] = squares(l, 0, planes, nothing)

    def await_following(picks):
        @pl.when(has_next)
        def _():
            for i in picks:
                backward_copies[i].wait_recv()

    await_following((0,))
    total = squares(images - 1, 1, last, nothing)
    await_following((1, 2))
    total = squares(images - 1, 0, 1, total)
    gbuf[me, images - 1 : images] = squares(images - 1, last, planes, total)

    def place(index):
        return {"img": index // n_gz, "gz": lax.rem(index, n_gz)}

    def g_copy(step):
        return pltpu.make_async_remote_copy(
            src_ref=gbuf.at[me],
            dst_ref=gbuf.at[me],
            send_sem=g_send.at[step],
            recv_sem=g_recv.at[step],
            device_id=place(lax.rem(me + step, n_all)),
            device_id_type=MESH,
        )

    def g_arrival(step):
        origin = lax.rem(me + n_all - step, n_all)
        return pltpu.make_async_remote_copy(
            src_ref=gbuf.at[origin],
            dst_ref=gbuf.at[origin],
            send_sem=g_send.at[step],
            recv_sem=g_recv.at[step],
            device_id=place(origin),
            device_id_type=MESH,
        )

    def g_start(step, carry):
        g_copy(step).start()
        return carry

    lax.fori_loop(1, n_all, g_start, 0, unroll=n_all <= 32)

    for copy in later_halos:
        copy.wait_recv()
    outer_planes(move_plane)

    @pl.when(has_previous)
    def _():
        for copy in forward_copies:
            copy.wait_recv()

    def g_wait(step, carry):
        g_arrival(step).wait_recv()
        return carry

    lax.fori_loop(1, n_all, g_wait, 0, unroll=n_all <= 32)

    total_images = images * n_img
    gaps = []
    for i in range(n_img):
        part = jnp.sum(gbuf[i * n_gz : (i + 1) * n_gz], axis=0)
        part = jnp.sum(part, axis=-1, keepdims=True)
        gaps.append(jnp.sqrt(part / cells + epsilon))

    def pick(low, high):
        out = jnp.zeros((1, 1), jnp.float32)
        for i in range(n_img):
            row = lax.broadcasted_iota(jnp.int32, (images, 1), 0) + i * images
            chosen = jnp.where((row >= low) & (row < high), gaps[i], 0.0)
            out = out + jnp.sum(chosen, axis=0, keepdims=True)
        return out

    length = pick(0, total_images - 1)
    for l in range(images):
        position = img * images + l
        arc = pick(0, position)
        target = length * (position.astype(jnp.float32) / (total_images - 1))
        gap_under = jnp.where(position == 0, 1.0, pick(position - 1, position))
        gap_over = jnp.where(position == total_images - 1, 1.0, pick(position, position + 1))
        back = jnp.clip((arc - target) / gap_under, 0.0, 1.0)
        ahead = jnp.clip((target - arc) / gap_over, 0.0, 1.0)
        weight_ref[l : l + 1] = jnp.broadcast_to(back, (1, ny))
        weight_ref[images + l : images + l + 1] = jnp.broadcast_to(ahead, (1, ny))

    for copy in first_halos + later_halos:
        copy.wait_send()
    for step in range(1, n_gz):
        h_copy(step).wait_send()

    @pl.when(has_previous)
    def _():
        for copy in backward_copies:
            copy.wait_send()

    @pl.when(has_next)
    def _():
        for copy in forward_copies:
            copy.wait_send()

    def g_done(step, carry):
        g_copy(step).wait_send()
        return carry

    lax.fori_loop(1, n_all, g_done, 0, unroll=n_all <= 32)


def finish(relaxed_ref, moved_ref, weight_ref, string_out, moved_out, string_buf, sem):
    images, planes = string_buf.shape[:2]
    moved_copy = pltpu.make_async_copy(moved_ref, moved_out, sem.at[images])
    moved_copy.start()
    copies = []
    for l in range(images):
        back, ahead = weight_ref[l : l + 1], weight_ref[images + l : images + l + 1]

        def blend(z, carry, l=l, back=back, ahead=ahead):
            current = relaxed_ref[l + 1, z].astype(jnp.float32)
            following = relaxed_ref[l + 2, z].astype(jnp.float32)
            previous = relaxed_ref[l, z].astype(jnp.float32)
            string_buf[l, z] = (
                current + ahead * (following - current) + back * (previous - current)
            ).astype(jnp.bfloat16)
            return carry

        lax.fori_loop(0, planes, blend, 0)
        copies.append(pltpu.make_async_copy(string_buf.at[l], string_out.at[l], sem.at[l]))
        copies[-1].start()
    for copy in copies + [moved_copy]:
        copy.wait()


def shards(ordering_variable, lattice_shift_field, eigenstrain_mismatch, thermal_state_kelvin):
    n_img, n_gz = lax.axis_size("img"), lax.axis_size("gz")
    images, planes, nx, ny = ordering_variable.shape
    dma = pltpu.SemaphoreType.DMA
    ordering_variable = pltpu.with_memory_space_constraint(ordering_variable, pltpu.HBM)
    lattice_shift_field = pltpu.with_memory_space_constraint(lattice_shift_field, pltpu.HBM)
    relaxed, moved, weights = pl.pallas_call(
        functools.partial(kernel, n_img, n_gz),
        out_shape=(
            jax.ShapeDtypeStruct((images + 2, planes, nx, ny), jnp.bfloat16),
            jax.ShapeDtypeStruct(lattice_shift_field.shape, jnp.bfloat16),
            jax.ShapeDtypeStruct((2 * images, ny), jnp.float32),
        ),
        in_specs=[
            pl.BlockSpec(memory_space=pltpu.SMEM),
            pl.BlockSpec(memory_space=pltpu.SMEM),
            pl.BlockSpec(memory_space=pltpu.HBM),
            pl.BlockSpec(memory_space=pltpu.HBM),
        ],
        out_specs=(pl.BlockSpec(memory_space=pltpu.VMEM),) * 3,
        scratch_shapes=[
            pltpu.VMEM((images, planes + 2, nx, ny), jnp.bfloat16),
            pltpu.VMEM((3, images, planes + 2, nx, ny), jnp.bfloat16),
            pltpu.VMEM((n_gz, images, LANES), jnp.float32),
            pltpu.VMEM((n_img * n_gz, images, LANES), jnp.float32),
            pltpu.SemaphoreType.REGULAR((n_img - 1,)),
            dma((2,)),
            dma((5,)),
            dma((5,)),
            dma((6,)),
            dma((6,)),
            dma((n_gz,)),
            dma((n_gz,)),
            dma((n_img * n_gz,)),
            dma((n_img * n_gz,)),
        ],
        compiler_params=pltpu.CompilerParams(
            collective_id=0, has_side_effects=True, vmem_limit_bytes=24 * 1024 * 1024
        ),
    )(eigenstrain_mismatch, thermal_state_kelvin, ordering_variable, lattice_shift_field)
    return pl.pallas_call(
        finish,
        out_shape=(
            jax.ShapeDtypeStruct(ordering_variable.shape, jnp.bfloat16),
            jax.ShapeDtypeStruct(lattice_shift_field.shape, jnp.bfloat16),
        ),
        in_specs=[pl.BlockSpec(memory_space=pltpu.VMEM)] * 3,
        out_specs=(pl.BlockSpec(memory_space=pltpu.HBM),) * 2,
        scratch_shapes=[pltpu.VMEM(ordering_variable.shape, jnp.bfloat16), dma((images + 1,))],
        compiler_params=pltpu.CompilerParams(vmem_limit_bytes=24 * 1024 * 1024),
    )(relaxed, moved, weights)


def solution(mesh):
    in_specs = (
        P(("grp", "img"), "gz", None, None),
        P(None, ("grp", "img"), "gz", None, None),
        P("grp"),
        P("grp"),
    )
    out_specs = (P(("grp", "img"), "gz", None, None), P(None, ("grp", "img"), "gz", None, None))
    return jax.shard_map(shards, mesh=mesh, in_specs=in_specs, out_specs=out_specs, check_vma=False)
```

```python
import functools

import jax
import jax.numpy as jnp
from jax import lax
from jax.experimental import pallas as pl
from jax.experimental.pallas import tpu as pltpu
from jax.sharding import PartitionSpec as P

stiff_eleven = 2.5
stiff_twelve = 1.5
stiff_shear = 1.2
barrier_height = 1.0
latent_enthalpy = 8.0
dissolution_limit_kelvin = 1250.0
gradient_coef = 1.0
mobility = 0.1
elastic_step = 0.03
epsilon = 1e-06
LANES = 128
MESH = pl.DeviceIdType.MESH


def switching(value):
    return value * value * (3.0 - 2.0 * value)


def roll(field, shift, axis):
    return pltpu.roll(field, shift % field.shape[axis], axis)


def ahead_of(field, axis):
    return roll(field, -1, axis) - field


def behind_of(field, axis):
    return field - roll(field, 1, axis)


def lane_row(field):
    row = jnp.sum(field, axis=0, keepdims=True)
    out = row[:, :LANES]
    for start in range(LANES, row.shape[1], LANES):
        out = out + row[:, start : start + LANES]
    return out


def kernel(
    n_img,
    n_gz,
    misfit_ref,
    kelvin_ref,
    order_in,
    shift_in,
    rbuf,
    moved_ref,
    weight_ref,
    obuf,
    sbuf,
    hbuf,
    gbuf,
    word_sem,
    load_sem,
    halo_send,
    halo_recv,
    image_send,
    image_recv,
    h_send,
    h_recv,
    g_send,
    g_recv,
):
    images, planes, nx, ny = order_in.shape
    cells = float(planes * n_gz * nx * ny)
    img = lax.axis_index("img")
    gz = lax.axis_index("gz")
    n_all = n_img * n_gz
    me = img * n_gz + gz

    def wrapped(index, count):
        return jnp.where(index >= count, index - count, index)

    gz_at = [wrapped(gz + step, n_gz) for step in range(n_gz)]
    img_at = [wrapped(img + step, n_img) for step in range(n_img)]
    above, below = gz_at[1 % n_gz], gz_at[-1]

    loads = [
        pltpu.make_async_copy(order_in, obuf.at[:, 1 : planes + 1], load_sem.at[0]),
        pltpu.make_async_copy(shift_in, sbuf.at[:, :, 1 : planes + 1], load_sem.at[1]),
    ]
    loads[0].start()

    barrier = pltpu.get_barrier_semaphore()

    has_next = img < n_img - 1
    has_previous = img > 0
    n_near = has_next.astype(jnp.int32) + has_previous.astype(jnp.int32)

    def signal_near(sem):
        @pl.when(has_next)
        def _():
            pl.semaphore_signal(sem, inc=1, device_id={"img": img + 1}, device_id_type=MESH)

        @pl.when(has_previous)
        def _():
            pl.semaphore_signal(sem, inc=1, device_id={"img": img - 1}, device_id_type=MESH)

    for step in range(1, n_gz):
        pl.semaphore_signal(
            barrier,
            inc=1,
            device_id={"gz": gz_at[step]},
            device_id_type=MESH,
        )
    signal_near(barrier)

    def spread(first, stop):
        for stage in range(first, stop):
            if stage > 0:
                pl.semaphore_wait(word_sem.at[stage - 1], n_near)
            if stage < n_img - 1:
                signal_near(word_sem.at[stage])

    def halo(slot, source, target, neighbour):
        return pltpu.make_async_remote_copy(
            src_ref=source,
            dst_ref=target,
            send_sem=halo_send.at[slot],
            recv_sem=halo_recv.at[slot],
            device_id={"gz": neighbour},
            device_id_type=MESH,
        )

    last, top = planes - 1, planes + 1
    order_down = halo(0, order_in.at[:, 0], obuf.at[:, top], below)
    order_up = halo(1, order_in.at[:, last], obuf.at[:, 0], above)
    lift_down = halo(2, shift_in.at[2, :, 0], sbuf.at[2, :, top], below)
    shift_up = halo(3, shift_in.at[:, :, last], sbuf.at[:, :, 0], above)
    flat_down = halo(4, shift_in.at[0:2, :, 0], sbuf.at[0:2, :, top], below)
    first_halos = (order_down, order_up, lift_down)
    later_halos = (shift_up, flat_down)

    misfit = misfit_ref[0]
    drive = latent_enthalpy * (kelvin_ref[0] - dissolution_limit_kelvin) / dissolution_limit_kelvin

    def order_at(l, z):
        return obuf[l, z].astype(jnp.float32)

    def shift_at(c, l, z):
        return sbuf[c, l, z].astype(jnp.float32)

    loads[0].wait()
    loads[1].start()
    for l in range(images):

        def add_h(z, total, l=l):
            return total + lane_row(switching(order_at(l, z + 1)))

        hbuf[gz, l : l + 1] = lax.fori_loop(0, planes, add_h, jnp.zeros((1, LANES), jnp.float32))

    pl.semaphore_wait(barrier, n_gz - 1 + n_near)
    spread(0, 1)

    def h_copy(step):
        return pltpu.make_async_remote_copy(
            src_ref=hbuf.at[gz],
            dst_ref=hbuf.at[gz],
            send_sem=h_send.at[step],
            recv_sem=h_recv.at[step],
            device_id={"gz": gz_at[step]},
            device_id_type=MESH,
        )

    def h_arrival(step):
        origin = gz_at[n_gz - step]
        return pltpu.make_async_remote_copy(
            src_ref=hbuf.at[origin],
            dst_ref=hbuf.at[origin],
            send_sem=h_send.at[step],
            recv_sem=h_recv.at[step],
            device_id={"gz": origin},
            device_id_type=MESH,
        )

    for step in range(1, n_gz):
        h_copy(step).start()
    for copy in first_halos:
        copy.start()
    spread(1, 2)

    def move_plane(l, z):
        ux, uy, uz = shift_at(0, l, z + 1), shift_at(1, l, z + 1), shift_at(2, l, z + 1)
        vx, vy, vz = shift_at(0, l, z), shift_at(1, l, z), shift_at(2, l, z)
        zx = shift_at(0, l, z + 2) - ux
        zy = shift_at(1, l, z + 2) - uy
        zz = shift_at(2, l, z + 2) - uz
        dx, dy, dz = ux - vx, uy - vy, uz - vz
        total = stiff_eleven + 2.0 * stiff_twelve
        swell = (-total * misfit) * switching(order_at(l, z + 1))
        swell_under = (-total * misfit) * switching(order_at(l, z))
        xx, yy = ahead_of(ux, 0), ahead_of(uy, 1)
        s_xx = stiff_eleven * xx + stiff_twelve * (yy + zz) + swell
        s_yy = stiff_eleven * yy + stiff_twelve * (xx + zz) + swell
        s_xy = stiff_shear * (ahead_of(uy, 0) + ahead_of(ux, 1))
        s_xz = stiff_shear * (ahead_of(uz, 0) + zx)
        s_yz = stiff_shear * (ahead_of(uz, 1) + zy)
        f_x = behind_of(s_xx, 0) + behind_of(s_xy, 1)
        f_x = f_x + stiff_shear * (ahead_of(dz, 0) + (zx - dx))
        moved_ref[0, l, z] = (ux + elastic_step * f_x).astype(jnp.bfloat16)
        f_y = behind_of(s_xy, 0) + behind_of(s_yy, 1)
        f_y = f_y + stiff_shear * (ahead_of(dz, 1) + (zy - dy))
        moved_ref[1, l, z] = (uy + elastic_step * f_y).astype(jnp.bfloat16)
        f_z = behind_of(s_xz, 0) + behind_of(s_yz, 1)
        f_z = f_z + stiff_eleven * (zz - dz)
        f_z = f_z + stiff_twelve * (ahead_of(dx, 0) + ahead_of(dy, 1)) + (swell - swell_under)
        moved_ref[2, l, z] = (uz + elastic_step * f_z).astype(jnp.bfloat16)

    def relax_plane(l, z, homogeneous):
        order = order_at(l, z + 1)
        uz = shift_at(2, l, z + 1)
        divergence = ahead_of(shift_at(0, l, z + 1), 0) + ahead_of(shift_at(1, l, z + 1), 1)
        divergence = divergence + (shift_at(2, l, z + 2) - uz)
        eigen = homogeneous - misfit * switching(order)
        trace = (stiff_eleven + 2.0 * stiff_twelve) * (divergence + 3.0 * eigen)
        laplace = order_at(l, z) + order_at(l, z + 2)
        laplace = laplace + (roll(order, 1, 0) + roll(order, -1, 0))
        laplace = laplace + (roll(order, 1, 1) + roll(order, -1, 1)) - 6.0 * order
        bend = order * (1.0 - order)
        potential = (
            bend * (barrier_height * 2.0 * (1.0 - 2.0 * order) + 6.0 * (drive - misfit * trace))
            - gradient_coef * laplace
        )
        rbuf[l + 1, z] = (order - mobility * potential).astype(jnp.bfloat16)

    inner = planes - 2

    def inner_planes(work):
        def one(step, carry):
            work(step // inner, lax.rem(step, inner) + 1)
            return carry

        lax.fori_loop(0, images * inner, one, 0)

    def outer_planes(work):
        def one(step, carry):
            work(step // 2, lax.rem(step, 2) * last)
            return carry

        lax.fori_loop(0, images * 2, one, 0)

    loads[1].wait()

    for step in range(1, n_gz):
        h_arrival(step).wait_recv()
    h_sum = jnp.sum(jnp.sum(hbuf[...], axis=0), axis=-1, keepdims=True)
    h_mean = misfit * (h_sum / cells)

    def relax(l, z):
        relax_plane(l, z, h_mean[l : l + 1])

    for l in range(images):

        def relax_inner(z, carry, l=l):
            relax(l, z)
            return carry

        lax.fori_loop(1, last, relax_inner, 0)

    def image_copy(slot, span, forward):
        return pltpu.make_async_remote_copy(
            src_ref=rbuf.at[images if forward else 1, span],
            dst_ref=rbuf.at[0 if forward else images + 1, span],
            send_sem=image_send.at[slot],
            recv_sem=image_recv.at[slot],
            device_id={"img": img + 1 if forward else img - 1},
            device_id_type=MESH,
        )

    spans = (slice(1, last), slice(0, 1), slice(last, planes))
    forward_copies = [image_copy(i, span, True) for i, span in enumerate(spans)]
    backward_copies = [image_copy(3 + i, span, False) for i, span in enumerate(spans)]

    def send_back(i):
        @pl.when(has_previous)
        def _():
            backward_copies[i].start()

    def send_on(i):
        @pl.when(has_next)
        def _():
            forward_copies[i].start()

    def send_images(picks):
        for i in picks:
            send_back(i)
            send_on(i)

    send_images((0,))
    spread(2, 3)

    @pl.when(jnp.logical_not(has_previous))
    def _():
        rbuf[0] = jnp.zeros_like(rbuf[0])

    @pl.when(jnp.logical_not(has_next))
    def _():
        rbuf[images + 1] = jnp.zeros_like(rbuf[images + 1])

    inner_planes(move_plane)

    order_up.wait_recv()
    for copy in later_halos:
        copy.start()
    relax(0, 0)
    send_back(1)
    for l in range(1, images):
        relax(l, 0)
    send_on(1)
    order_down.wait_recv()
    lift_down.wait_recv()
    relax(0, last)
    send_back(2)
    for l in range(1, images):
        relax(l, last)
    send_on(2)
    spread(3, n_img)

    def squares(l, first, stop, total):
        def add(z, total):
            step = rbuf[l + 2, z].astype(jnp.float32) - rbuf[l + 1, z].astype(jnp.float32)
            return total + lane_row(step * step)

        return lax.fori_loop(first, stop, add, total)

    nothing = jnp.zeros((1, LANES), jnp.float32)
    for l in range(images - 1):
        gbuf[me, l : l + 1] = squares(l, 0, planes, nothing)

    def await_following(picks):
        @pl.when(has_next)
        def _():
            for i in picks:
                backward_copies[i].wait_recv()

    await_following((0,))
    total = squares(images - 1, 1, last, nothing)
    await_following((1, 2))
    total = squares(images - 1, 0, 1, total)
    gbuf[me, images - 1 : images] = squares(images - 1, last, planes, total)

    def g_copy(to_img, to_gz):
        return pltpu.make_async_remote_copy(
            src_ref=gbuf.at[me],
            dst_ref=gbuf.at[me],
            send_sem=g_send.at[0],
            recv_sem=g_recv.at[0],
            device_id={"img": to_img, "gz": to_gz},
            device_id_type=MESH,
        )

    if n_all <= 32:
        for far in range(n_img - 1, -1, -1):
            for near in range(n_gz - 1, -1, -1):
                if far + near > 0:
                    g_copy(img_at[far], gz_at[near]).start()
    else:

        def g_start(step, carry):
            other = lax.rem(me + step, n_all)
            g_copy(lax.div(other, n_gz), lax.rem(other, n_gz)).start()
            return carry

        lax.fori_loop(1, n_all, g_start, 0)

    g_rows = pltpu.make_async_remote_copy(
        src_ref=gbuf.at[0 : n_all - 1],
        dst_ref=gbuf.at[0 : n_all - 1],
        send_sem=g_send.at[0],
        recv_sem=g_recv.at[0],
        device_id={"gz": above},
        device_id_type=MESH,
    )

    for copy in later_halos:
        copy.wait_recv()
    outer_planes(move_plane)

    @pl.when(has_previous)
    def _():
        for copy in forward_copies:
            copy.wait_recv()

    g_rows.wait_recv()

    total_images = images * n_img
    gaps = []
    for i in range(n_img):
        part = jnp.sum(gbuf[i * n_gz : (i + 1) * n_gz], axis=0)
        part = jnp.sum(part, axis=-1, keepdims=True)
        gaps.append(jnp.sqrt(part / cells + epsilon))

    def pick(low, high):
        out = jnp.zeros((1, 1), jnp.float32)
        for i in range(n_img):
            row = lax.broadcasted_iota(jnp.int32, (images, 1), 0) + i * images
            chosen = jnp.where((row >= low) & (row < high), gaps[i], 0.0)
            out = out + jnp.sum(chosen, axis=0, keepdims=True)
        return out

    length = pick(0, total_images - 1)
    for l in range(images):
        position = img * images + l
        arc = pick(0, position)
        target = length * (position.astype(jnp.float32) / (total_images - 1))
        gap_under = jnp.where(position == 0, 1.0, pick(position - 1, position))
        gap_over = jnp.where(position == total_images - 1, 1.0, pick(position, position + 1))
        back = jnp.clip((arc - target) / gap_under, 0.0, 1.0)
        ahead = jnp.clip((target - arc) / gap_over, 0.0, 1.0)
        weight_ref[l : l + 1] = jnp.broadcast_to(back, (1, ny))
        weight_ref[images + l : images + l + 1] = jnp.broadcast_to(ahead, (1, ny))

    for copy in first_halos + later_halos:
        copy.wait_send()
    for step in range(1, n_gz):
        h_copy(step).wait_send()

    @pl.when(has_previous)
    def _():
        for copy in backward_copies:
            copy.wait_send()

    @pl.when(has_next)
    def _():
        for copy in forward_copies:
            copy.wait_send()

    g_rows.wait_send()


def finish(relaxed_ref, moved_ref, weight_ref, string_out, moved_out, string_buf, sem):
    images, planes = string_buf.shape[:2]
    moved_copy = pltpu.make_async_copy(moved_ref, moved_out, sem.at[images])
    moved_copy.start()
    copies = []
    for l in range(images):
        back, ahead = weight_ref[l : l + 1], weight_ref[images + l : images + l + 1]

        def blend(z, carry, l=l, back=back, ahead=ahead):
            current = relaxed_ref[l + 1, z].astype(jnp.float32)
            following = relaxed_ref[l + 2, z].astype(jnp.float32)
            previous = relaxed_ref[l, z].astype(jnp.float32)
            string_buf[l, z] = (
                current + ahead * (following - current) + back * (previous - current)
            ).astype(jnp.bfloat16)
            return carry

        lax.fori_loop(0, planes, blend, 0)
        copies.append(pltpu.make_async_copy(string_buf.at[l], string_out.at[l], sem.at[l]))
        copies[-1].start()
    for copy in copies + [moved_copy]:
        copy.wait()


def shards(ordering_variable, lattice_shift_field, eigenstrain_mismatch, thermal_state_kelvin):
    n_img, n_gz = lax.axis_size("img"), lax.axis_size("gz")
    images, planes, nx, ny = ordering_variable.shape
    dma = pltpu.SemaphoreType.DMA
    ordering_variable = pltpu.with_memory_space_constraint(ordering_variable, pltpu.HBM)
    lattice_shift_field = pltpu.with_memory_space_constraint(lattice_shift_field, pltpu.HBM)
    relaxed, moved, weights = pl.pallas_call(
        functools.partial(kernel, n_img, n_gz),
        out_shape=(
            jax.ShapeDtypeStruct((images + 2, planes, nx, ny), jnp.bfloat16),
            jax.ShapeDtypeStruct(lattice_shift_field.shape, jnp.bfloat16),
            jax.ShapeDtypeStruct((2 * images, ny), jnp.float32),
        ),
        in_specs=[
            pl.BlockSpec(memory_space=pltpu.SMEM),
            pl.BlockSpec(memory_space=pltpu.SMEM),
            pl.BlockSpec(memory_space=pltpu.HBM),
            pl.BlockSpec(memory_space=pltpu.HBM),
        ],
        out_specs=(pl.BlockSpec(memory_space=pltpu.VMEM),) * 3,
        scratch_shapes=[
            pltpu.VMEM((images, planes + 2, nx, ny), jnp.bfloat16),
            pltpu.VMEM((3, images, planes + 2, nx, ny), jnp.bfloat16),
            pltpu.VMEM((n_gz, images, LANES), jnp.float32),
            pltpu.VMEM((n_img * n_gz, images, LANES), jnp.float32),
            pltpu.SemaphoreType.REGULAR((n_img - 1,)),
            dma((2,)),
            dma((5,)),
            dma((5,)),
            dma((6,)),
            dma((6,)),
            dma((n_gz,)),
            dma((n_gz,)),
            dma((1,)),
            dma((1,)),
        ],
        compiler_params=pltpu.CompilerParams(
            collective_id=0, has_side_effects=True, vmem_limit_bytes=24 * 1024 * 1024
        ),
    )(eigenstrain_mismatch, thermal_state_kelvin, ordering_variable, lattice_shift_field)
    return pl.pallas_call(
        finish,
        out_shape=(
            jax.ShapeDtypeStruct(ordering_variable.shape, jnp.bfloat16),
            jax.ShapeDtypeStruct(lattice_shift_field.shape, jnp.bfloat16),
        ),
        in_specs=[pl.BlockSpec(memory_space=pltpu.VMEM)] * 3,
        out_specs=(pl.BlockSpec(memory_space=pltpu.HBM),) * 2,
        scratch_shapes=[pltpu.VMEM(ordering_variable.shape, jnp.bfloat16), dma((images + 1,))],
        compiler_params=pltpu.CompilerParams(vmem_limit_bytes=24 * 1024 * 1024),
    )(relaxed, moved, weights)


def solution(mesh):
    in_specs = (
        P(("grp", "img"), "gz", None, None),
        P(None, ("grp", "img"), "gz", None, None),
        P("grp"),
        P("grp"),
    )
    out_specs = (P(("grp", "img"), "gz", None, None), P(None, ("grp", "img"), "gz", None, None))
    return jax.shard_map(shards, mesh=mesh, in_specs=in_specs, out_specs=out_specs, check_vma=False)
```
